32 devices in a mesh: seq: 4 (over z), head: 2 (over y), dp: 4 (over x, core).
Axes of the slice: x: 2, y: 2, z: 4, core: 2. Of those that a mesh axis runs over, the one named last changes fastest.
Arguments:
- layer_input: bfloat16 [4, 512, 6144], P('dp', 'seq'), may hold values from -6 to 6
- queries: bfloat16 [4, 512, 1024], P('dp', 'seq', 'head'), may hold values from -6 to 6
- key_rows: bfloat16 [4, 512, 1024], P('dp', 'seq', 'head'), may hold values from -6 to 6
- value_rows: bfloat16 [4, 512, 1024], P('dp', 'seq', 'head'), may hold values from -6 to 6
- grad_out: bfloat16 [4, 512, 1024], P('dp', 'seq', 'head'), may hold values from -6 to 6
- log_decay: float32 [4, 512, 8], P('dp', 'seq', 'head'), may hold values from -2 to 0, as said below
Outputs:
- grad_query: bfloat16 [4, 512, 1024], P('dp', 'seq', 'head')
- grad_key: bfloat16 [4, 512, 1024], P('dp', 'seq', 'head')
- grad_value: bfloat16 [4, 512, 1024], P('dp', 'seq', 'head')
- key_weight_grad: bfloat16 [6144, 1024], P('seq', 'head')
- value_weight_grad: bfloat16 [6144, 1024], P('seq', 'head')
The draws below stay inside these ranges and needn't reach their ends.
Inputs may be any that keep to these rules, and one draw needn't show every extreme that they name: log_decay is never positive.
All inputs are finite; a program needn't handle non-finite values.
Results may differ from the reference program's by a relative error of at most 0.0062.
Values may be sent and summed in bfloat16 or wider, within the bound.
A program may use at most 64 MiB of HBM per device.

```python
import math
import jax
import jax.numpy as jnp
from jax import lax

D = 6144
DH = 128
HALF_HEADS = 8
TOK_DEV = 128
SEQUENCE_LENGTH = 512
SEQUENCE_COUNT = 4


def draw_log_decay(key, part):
    random_key_splits = jax.random.split(key, 7)
    fast_share = 5
    fast_heads = jax.random.randint(random_key_splits[0], (HALF_HEADS,), 0, 10) < fast_share
    fast_rate = jnp.exp(jax.random.uniform(random_key_splits[1], (HALF_HEADS,), jnp.float32, math.log(2.5 / TOK_DEV), math.log(4.0 / TOK_DEV)))
    slow_rate = jnp.exp(jax.random.uniform(random_key_splits[2], (HALF_HEADS,), jnp.float32, math.log(0.05 / SEQUENCE_LENGTH), math.log(0.4 / SEQUENCE_LENGTH)))
    head_decay_speed = jnp.where(fast_heads, fast_rate, slow_rate)
    jitter_level = jnp.exp(jax.random.uniform(random_key_splits[3], (SEQUENCE_COUNT, SEQUENCE_LENGTH, HALF_HEADS), jnp.float32, -math.log(2.0), math.log(2.0)))
    block_multiplier = jnp.exp(jax.random.uniform(random_key_splits[4], (SEQUENCE_COUNT, SEQUENCE_LENGTH // TOK_DEV, 1, HALF_HEADS), jnp.float32, -math.log(2.0), math.log(2.0)))
    block_multiplier = jnp.broadcast_to(block_multiplier, (SEQUENCE_COUNT, SEQUENCE_LENGTH // TOK_DEV, TOK_DEV, HALF_HEADS)).reshape(SEQUENCE_COUNT, SEQUENCE_LENGTH, HALF_HEADS)
    spike_positions = jax.random.randint(random_key_splits[5], (SEQUENCE_COUNT, 3), 0, SEQUENCE_LENGTH)
    spike_mask = jnp.any(jnp.arange(SEQUENCE_LENGTH)[None, :, None] == spike_positions[:, None, :], axis=2)
    spike_strength = jax.random.uniform(random_key_splits[6], (SEQUENCE_COUNT, SEQUENCE_LENGTH, HALF_HEADS), jnp.float32, math.log(0.6), math.log(0.8))
    return -head_decay_speed[None, None, :] * jitter_level * block_multiplier + jnp.where(spike_mask[:, :, None], spike_strength, 0.0)


def spiked(entries, stream_key, source, target, parts, factor):
    def block_of(dim):
        return (jnp.arange(entries.shape[dim]) // (entries.shape[dim] // parts)).reshape((-1,) + (1,) * (entries.ndim - 1 - dim))

    near = jax.random.permutation(stream_key, parts)[block_of(target)]
    second = (block_of(target) + parts // 2) % parts
    return jnp.where((block_of(source) == near) | (block_of(source) == second), factor * entries, entries)


def block_levels(stream_key, shape, cuts, smallest, top_value):
    def one(axis_at, blocks):
        draws = jax.random.uniform(jax.random.fold_in(jax.random.fold_in(stream_key, 6), axis_at), (blocks,), jnp.float32, smallest / len(cuts), top_value / len(cuts))
        return jnp.repeat(jnp.exp(draws), shape[axis_at] // blocks).reshape((-1,) + (1,) * (len(shape) - axis_at - 1))

    level = one(*cuts[0])
    for cut in cuts[1:]:
        level = level * one(*cut)
    return level


def centred(rng, dims, deviation, most, cuts=(), kind=jnp.bfloat16):
    drawn = deviation * jax.random.normal(rng, dims, jnp.float32)
    if cuts:
        drawn = drawn * block_levels(rng, dims, cuts, -0.22, 0.18)
    return jnp.clip(drawn, -most, most).astype(kind)


def bell_draw_with(own_key, shape, deviation, most, cuts, heavy, kind=jnp.bfloat16):
    result = deviation * jax.random.normal(own_key, shape, jnp.float32)
    if cuts:
        result = result * block_levels(own_key, shape, cuts, -0.22, 0.18)
    return jnp.clip(spiked(result, jax.random.fold_in(own_key, 3), *heavy), -most, most).astype(kind)


def setup_inputs(seed: int = 0) -> dict:
    keys = jax.random.split(jax.random.key(seed), 7)
    return {
        "layer_input": bell_draw_with(keys[0], (SEQUENCE_COUNT, SEQUENCE_LENGTH, D), 1.0, 6.0, ((0, 4), (1, 4)), (1, 2, 4, 2.0)),
        "queries": centred(keys[1], (SEQUENCE_COUNT, SEQUENCE_LENGTH, HALF_HEADS * DH), 1.0, 6.0, ((0, 4), (1, 4), (2, 2))),
        "key_rows": centred(keys[2], (SEQUENCE_COUNT, SEQUENCE_LENGTH, HALF_HEADS * DH), 1.0, 6.0, ((0, 4), (1, 4), (2, 2))),
        "value_rows": centred(keys[3], (SEQUENCE_COUNT, SEQUENCE_LENGTH, HALF_HEADS * DH), 1.0, 6.0, ((0, 4), (1, 4), (2, 2))),
        "grad_out": centred(keys[4], (SEQUENCE_COUNT, SEQUENCE_LENGTH, HALF_HEADS * DH), 1.0, 6.0, ((0, 4), (1, 4), (2, 2))),
        "log_decay": draw_log_decay(jax.random.fold_in(keys[6], 71), 0),
    }


top_precision = lax.Precision.HIGHEST

def carry_step(carried, item):
    state, total = item
    return (jnp.exp(total) * carried + state, carried)

def product(form, left, right):
    return jnp.einsum(form, left.astype(jnp.float32), right.astype(jnp.float32), precision=top_precision)

def one_head(inputs):
    query_head, key_head, value_head, grad_head, decay_head = inputs
    blocks = SEQUENCE_LENGTH // TOK_DEV
    query_blocks = query_head.reshape(blocks, TOK_DEV, DH)
    key_blocks = key_head.reshape(blocks, TOK_DEV, DH)
    value_blocks = value_head.reshape(blocks, TOK_DEV, DH)
    grad_blocks = grad_head.reshape(blocks, TOK_DEV, DH)
    running = jnp.cumsum(decay_head.reshape(blocks, TOK_DEV), axis=1)
    totals = running[:, -1]
    positions = jnp.arange(TOK_DEV)
    lower_mask = positions[:, None] >= positions[None, :]
    decay_mask = jnp.where(lower_mask[None], jnp.exp(jnp.minimum(running[:, :, None] - running[:, None, :], 0.0)), 0.0)
    to_end = jnp.exp(totals[:, None] - running)
    from_start = jnp.exp(running)
    key_rows_scaled = (key_blocks * to_end[:, :, None]).astype(jnp.bfloat16)
    scaled_queries = (query_blocks * from_start[:, :, None]).astype(jnp.bfloat16)
    key_state = product('btk,btv->bkv', key_rows_scaled, value_blocks)
    query_state = product('btq,btv->bqv', scaled_queries, grad_blocks)
    empty = jnp.zeros((DH, DH), jnp.float32)
    unused, prefix_running = lax.scan(carry_step, empty, (key_state, totals))
    unused, suffix = lax.scan(carry_step, empty, (query_state, totals), reverse=True)
    prefix_reduced = prefix_running.astype(jnp.bfloat16)
    suffix_low = suffix.astype(jnp.bfloat16)
    value_weights = (product('btv,bjv->btj', grad_blocks, value_blocks) * decay_mask).astype(jnp.bfloat16)
    key_weights = (product('btq,bjq->btj', query_blocks, key_blocks) * decay_mask).astype(jnp.bfloat16)
    scale = 1.0 / DH
    grad_query = (product('btj,bjk->btk', value_weights, key_blocks) + from_start[:, :, None] * product('bkv,btv->btk', prefix_reduced, grad_blocks)) * scale
    grad_key = (product('btj,btq->bjq', value_weights, query_blocks) + to_end[:, :, None] * product('bqv,bjv->bjq', suffix_low, value_blocks)) * scale
    grad_value = (product('btj,btv->bjv', key_weights, grad_blocks) + to_end[:, :, None] * product('bqv,bjq->bjv', suffix_low, key_blocks)) * scale
    return (grad_query.reshape(SEQUENCE_LENGTH, DH), grad_key.reshape(SEQUENCE_LENGTH, DH), grad_value.reshape(SEQUENCE_LENGTH, DH))

def heads_major(array):
    return array.reshape(SEQUENCE_COUNT, SEQUENCE_LENGTH, HALF_HEADS, DH).transpose(0, 2, 1, 3).reshape(SEQUENCE_COUNT * HALF_HEADS, SEQUENCE_LENGTH, DH)

def tokens_major(array):
    return array.reshape(SEQUENCE_COUNT, HALF_HEADS, SEQUENCE_LENGTH, DH).transpose(0, 2, 1, 3).reshape(SEQUENCE_COUNT, SEQUENCE_LENGTH, HALF_HEADS * DH).astype(jnp.bfloat16)

def weight_grad(flat_input, gradient):
    factor = 1.0 / math.sqrt(SEQUENCE_COUNT * SEQUENCE_LENGTH)
    summed = lax.dot_general(flat_input, gradient.reshape(SEQUENCE_COUNT * SEQUENCE_LENGTH, HALF_HEADS * DH), (((0,), (0,)), ((), ())), preferred_element_type=jnp.float32)
    return (summed * factor).astype(jnp.bfloat16)

def reference(layer_input, queries, key_rows, value_rows, grad_out, log_decay):
    decays = log_decay.transpose(0, 2, 1).reshape(SEQUENCE_COUNT * HALF_HEADS, SEQUENCE_LENGTH)
    query_grads, key_grads, value_grads = lax.map(one_head, (heads_major(queries), heads_major(key_rows), heads_major(value_rows), heads_major(grad_out), decays))
    grad_query = tokens_major(query_grads)
    grad_key = tokens_major(key_grads)
    grad_value = tokens_major(value_grads)
    flat_input = layer_input.reshape(SEQUENCE_COUNT * SEQUENCE_LENGTH, D)
    key_weight_grad = weight_grad(flat_input, grad_key)
    value_weight_grad = weight_grad(flat_input, grad_value)
    return (grad_query, grad_key, grad_value, key_weight_grad, value_weight_grad)
```

```python
import functools
import math

import jax
import jax.numpy as jnp
from jax import lax
from jax.experimental import pallas as pl
from jax.experimental.pallas import tpu as pltpu
from jax.sharding import PartitionSpec as P

DH = 128
CHUNKS = 2
MESH = pl.DeviceIdType.MESH
BF16 = jnp.bfloat16
F32 = jnp.float32


def dot(left, right, dims):
    return lax.dot_general(left, right, (dims, ((), ())), preferred_element_type=F32)


NN = ((1,), (0,))
NT = ((1,), (1,))
TN = ((0,), (0,))


def kernel(
    n, bits, heads, factor,
    x_hbm, q_ref, k_ref, v_ref, g_ref, ld_ref,
    gq_ref, gk_ref, gv_ref, ok_ref, ov_ref,
    cum_s, tot_s, kst_own, qst_own, kst, qst, tot_b, tot_a, w_b, w_a, pre, suf,
    acc_q, acc_k, acc_v, rx, rxt, gg, half_send, half_recv, mine, lev_send, lev_recv,
    st_send, st_recv, x_send, x_recv, x_sem, g_send, g_recv,
    c_send, c_recv, l_send, l_recv, f_send, f_recv,
):
    s = lax.axis_index("seq")
    d = lax.axis_index("dp")
    length = q_ref.shape[0]
    cols = rx.shape[2]
    half = cols // 2
    size = half // CHUNKS
    outs = (ok_ref, ov_ref)

    def partner(bit):
        block = 1 << bit
        low = lax.rem(lax.div(d, block), 2)
        return d + block - 2 * block * low

    near = partner(0)
    barrier = pltpu.get_barrier_semaphore()
    for step in range(1, n):
        pl.semaphore_signal(
            barrier, inc=1, device_id={"seq": lax.rem(s + step, n)}, device_id_type=MESH
        )
    for bit in range(bits):
        pl.semaphore_signal(barrier, inc=1, device_id={"dp": partner(bit)}, device_id_type=MESH)

    row = lax.broadcasted_iota(jnp.int32, (length, length), 0)
    col = lax.broadcasted_iota(jnp.int32, (length, length), 1)
    lower = row >= col
    tri = jnp.where(lower, 1.0, 0.0).astype(F32)
    tot_s[...] = jnp.zeros_like(tot_s)
    for h in range(heads):
        at = pl.ds(h * DH, DH)
        decays = jnp.broadcast_to(ld_ref[:, h : h + 1], (length, DH))
        cum = lax.dot_general(
            tri, decays, (NN, ((), ())), precision=lax.Precision.HIGHEST, preferred_element_type=F32
        )
        cum_s[h] = cum
        total = cum[length - 1 : length, :]
        tot_s[h : h + 1, :] = total
        keys = (k_ref[:, at].astype(F32) * jnp.exp(total - cum)).astype(BF16)
        queries = (q_ref[:, at].astype(F32) * jnp.exp(cum)).astype(BF16)
        kst_own[h] = dot(keys, v_ref[:, at], TN).astype(BF16)
        qst_own[h] = dot(queries, g_ref[:, at], TN).astype(BF16)

    pl.semaphore_wait(barrier, n - 1 + bits)

    def send(kind, step, src, dst, peer):
        return pltpu.make_async_remote_copy(
            src_ref=src, dst_ref=dst, send_sem=st_send.at[kind, step - 1],
            recv_sem=st_recv.at[kind, step - 1], device_id={"seq": peer}, device_id_type=MESH,
        )

    def forward(step):
        peer = lax.rem(s + step, n)
        return (
            send(0, step, tot_s, tot_b.at[step - 1], peer),
            send(1, step, kst_own, kst.at[step - 1], peer),
        )

    def backward(step):
        peer = lax.rem(s + n - step, n)
        return (
            send(2, step, tot_s, tot_a.at[step - 1], peer),
            send(3, step, qst_own, qst.at[step - 1], peer),
        )

    for step in range(n - 1, 0, -1):
        @pl.when(s + step < n)
        def _(step=step):
            for copy in forward(step):
                copy.start()

        @pl.when(s >= step)
        def _(step=step):
            for copy in backward(step):
                copy.start()

    x_own = pltpu.make_async_copy(
        x_hbm.at[:, pl.ds(pl.multiple_of(s * cols, 128), cols)], rx.at[0], x_sem
    )
    x_own.start()
    x_copies = []
    for step in range(1, n):
        peer = lax.rem(s + step, n)
        copy = pltpu.make_async_remote_copy(
            src_ref=x_hbm.at[:, pl.ds(pl.multiple_of(peer * cols, 128), cols)],
            dst_ref=rx.at[step], send_sem=x_send.at[step - 1], recv_sem=x_recv.at[step - 1],
            device_id={"seq": peer}, device_id_type=MESH,
        )
        copy.start()
        x_copies.append(copy)

    for h in range(heads):
        at = pl.ds(h * DH, DH)
        cum = cum_s[h]
        mask = jnp.where(lower, jnp.exp(jnp.minimum(cum - cum.T, 0.0)), 0.0)
        q, k, v, g = q_ref[:, at], k_ref[:, at], v_ref[:, at], g_ref[:, at]
        value_weights = (dot(g, v, NT) * mask).astype(BF16)
        key_weights = (dot(q, k, NT) * mask).astype(BF16)
        acc_q[:, at] = dot(value_weights, k, NN)
        acc_k[:, at] = dot(value_weights, q, TN)
        acc_v[:, at] = dot(key_weights, g, TN)

    for ref in (pre, suf, w_b, w_a):
        ref[...] = jnp.zeros_like(ref)
    for step in range(1, n):
        @pl.when(s + step < n)
        def _(step=step):
            for copy in backward(step):
                copy.wait_recv()
            weight = jnp.exp(w_a[...])
            for h in range(heads):
                suf[h] += weight[h : h + 1, :] * qst[step - 1, h].astype(F32)
            w_a[...] += tot_a[step - 1]

        @pl.when(s >= step)
        def _(step=step):
            for copy in forward(step):
                copy.wait_recv()
            weight = jnp.exp(w_b[...])
            for h in range(heads):
                pre[h] += weight[h : h + 1, :] * kst[step - 1, h].astype(F32)
            w_b[...] += tot_b[step - 1]

    scale = 1.0 / DH
    g_copies = []

    def spread(part):
        copies = []
        for step in range(n - 1, 0, -1):
            copy = pltpu.make_async_remote_copy(
                src_ref=gg.at[part, 0], dst_ref=gg.at[part, step],
                send_sem=g_send.at[part, step - 1], recv_sem=g_recv.at[part, step - 1],
                device_id={"seq": lax.rem(s + step, n)}, device_id_type=MESH,
            )
            copy.start()
            copies.append(copy)
        g_copies.append(copies)

    for h in range(heads):
        at = pl.ds(h * DH, DH)
        cum = cum_s[h]
        to_end = jnp.exp(cum[length - 1 : length, :] - cum)
        carried = to_end * dot(v_ref[:, at], suf[h].astype(BF16), NT)
        gg[0, 0, :, at] = ((acc_k[:, at] + carried) * scale).astype(BF16)
    spread(0)
    for h in range(heads):
        at = pl.ds(h * DH, DH)
        cum = cum_s[h]
        to_end = jnp.exp(cum[length - 1 : length, :] - cum)
        carried = to_end * dot(k_ref[:, at], suf[h].astype(BF16), NN)
        gg[1, 0, :, at] = ((acc_v[:, at] + carried) * scale).astype(BF16)
    spread(1)
    for h in range(heads):
        at = pl.ds(h * DH, DH)
        carried = jnp.exp(cum_s[h]) * dot(g_ref[:, at], pre[h].astype(BF16), NT)
        gq_ref[:, at] = ((acc_q[:, at] + carried) * scale).astype(BF16)
    gk_ref[...] = gg[0, 0]
    gv_ref[...] = gg[1, 0]

    for step in range(n):
        if step == 0:
            x_own.wait()
        else:
            x_copies[step - 1].wait_recv()
        rxt[:, step * length : (step + 1) * length] = rx[step].T

    low = lax.rem(d, 2)
    own_row = low * half
    far_row = (1 - low) * half

    def product(start, part):
        rows = rxt[pl.ds(pl.multiple_of(start, 16), size), :]
        return dot(rows, gg[part].reshape(n * length, gg.shape[3]), NN)

    def exchange(src, dst, send_sem, recv_sem, to):
        return pltpu.make_async_remote_copy(
            src_ref=src, dst_ref=dst, send_sem=send_sem, recv_sem=recv_sem,
            device_id={"dp": to}, device_id_type=MESH,
        )

    halves, levels, finals = {}, {}, {}
    for part in range(2):
        for copy in g_copies[part]:
            copy.wait_recv()
        for i in range(CHUNKS):
            half_send[part, i] = product(far_row + i * size, part).astype(BF16)
            halves[part, i] = exchange(
                half_send.at[part, i], half_recv.at[part, i],
                c_send.at[part, i], c_recv.at[part, i], near,
            )
            halves[part, i].start()
        for i in range(CHUNKS):
            total = product(own_row + i * size, part)
            halves[part, i].wait_recv()
            total = total + half_recv[part, i].astype(F32)
            lev_send[0, part, i] = total.astype(BF16)
            levels[0, part, i] = exchange(
                lev_send.at[0, part, i], lev_recv.at[0, part, i],
                l_send.at[0, part, i], l_recv.at[0, part, i], partner(1),
            )
            levels[0, part, i].start()
    for level in range(bits - 1):
        for part in range(2):
            for i in range(CHUNKS):
                levels[level, part, i].wait_recv()
                total = lev_send[level, part, i].astype(F32) + lev_recv[level, part, i].astype(F32)
                if level < bits - 2:
                    lev_send[level + 1, part, i] = total.astype(BF16)
                    levels[level + 1, part, i] = exchange(
                        lev_send.at[level + 1, part, i], lev_recv.at[level + 1, part, i],
                        l_send.at[level + 1, part, i], l_recv.at[level + 1, part, i],
                        partner(level + 2),
                    )
                    levels[level + 1, part, i].start()
                    continue
                here = outs[part].at[pl.ds(pl.multiple_of(own_row + i * size, 16), size), :]
                here[...] = (total * factor).astype(BF16)
                finals[part, i] = exchange(
                    here, here, f_send.at[part, i], f_recv.at[part, i], near
                )
                finals[part, i].start()

    for step in range(1, n):
        @pl.when(s + step < n)
        def _(step=step):
            for copy in forward(step):
                copy.wait_send()

        @pl.when(s >= step)
        def _(step=step):
            for copy in backward(step):
                copy.wait_send()
    for copy in x_copies + g_copies[0] + g_copies[1] + list(halves.values()) + list(levels.values()):
        copy.wait_send()
    for copy in finals.values():
        copy.wait()


def per_device(layer_input, queries, key_rows, value_rows, grad_out, log_decay):
    n = lax.axis_size("seq")
    dp = lax.axis_size("dp")
    bits = dp.bit_length() - 1
    length, width = queries.shape[1:]
    heads = log_decay.shape[2]
    features = layer_input.shape[2]
    cols = features // n
    size = cols // 2 // CHUNKS
    tot_rows = -(-heads // 8) * 8
    factor = 1.0 / math.sqrt(dp * n * length)
    vmem = pl.BlockSpec(memory_space=pltpu.VMEM)
    dma = pltpu.SemaphoreType.DMA
    tile = (heads, DH, DH)
    grads = pl.pallas_call(
        functools.partial(kernel, n, bits, heads, factor),
        out_shape=[jax.ShapeDtypeStruct((length, width), BF16)] * 3
        + [jax.ShapeDtypeStruct((cols, width), BF16)] * 2,
        in_specs=[pl.BlockSpec(memory_space=pl.ANY)] + [vmem] * 5,
        out_specs=[vmem] * 5,
        scratch_shapes=[
            pltpu.VMEM((heads, length, DH), F32),
            pltpu.VMEM((tot_rows, DH), F32),
            pltpu.VMEM(tile, BF16),
            pltpu.VMEM(tile, BF16),
            pltpu.VMEM((n - 1,) + tile, BF16),
            pltpu.VMEM((n - 1,) + tile, BF16),
            pltpu.VMEM((n - 1, tot_rows, DH), F32),
            pltpu.VMEM((n - 1, tot_rows, DH), F32),
            pltpu.VMEM((tot_rows, DH), F32),
            pltpu.VMEM((tot_rows, DH), F32),
            pltpu.VMEM(tile, F32),
            pltpu.VMEM(tile, F32),
            pltpu.VMEM((length, width), F32),
            pltpu.VMEM((length, width), F32),
            pltpu.VMEM((length, width), F32),
            pltpu.VMEM((n, length, cols), BF16),
            pltpu.VMEM((cols, n * length), BF16),
            pltpu.VMEM((2, n, length, width), BF16),
            pltpu.VMEM((2, CHUNKS, size, width), BF16),
            pltpu.VMEM((2, CHUNKS, size, width), BF16),
            pltpu.VMEM((8, 128), F32),
            pltpu.VMEM((bits - 1, 2, CHUNKS, size, width), BF16),
            pltpu.VMEM((bits - 1, 2, CHUNKS, size, width), BF16),
            dma((4, n - 1)), dma((4, n - 1)),
            dma((n - 1,)), dma((n - 1,)), dma,
            dma((2, n - 1)), dma((2, n - 1)),
            dma((2, CHUNKS)), dma((2, CHUNKS)),
            dma((bits - 1, 2, CHUNKS)), dma((bits - 1, 2, CHUNKS)),
            dma((2, CHUNKS)), dma((2, CHUNKS)),
        ],
        compiler_params=pltpu.CompilerParams(
            collective_id=0, has_side_effects=True, vmem_limit_bytes=48 << 20
        ),
    )(layer_input[0], queries[0], key_rows[0], value_rows[0], grad_out[0], log_decay[0])
    return (grads[0][None], grads[1][None], grads[2][None], grads[3], grads[4])


def solution(mesh):
    return jax.shard_map(
        per_device,
        mesh=mesh,
        in_specs=(
            P("dp", "seq", None),
            P("dp", "seq", "head"),
            P("dp", "seq", "head"),
            P("dp", "seq", "head"),
            P("dp", "seq", "head"),
            P("dp", "seq", "head"),
        ),
        out_specs=(
            P("dp", "seq", "head"),
            P("dp", "seq", "head"),
            P("dp", "seq", "head"),
            P("seq", "head"),
            P("seq", "head"),
        ),
        check_vma=False,
    )
```

```python
import functools
import math

import jax
import jax.numpy as jnp
from jax import lax
from jax.experimental import pallas as pl
from jax.experimental.pallas import tpu as pltpu
from jax.sharding import PartitionSpec as P

DH = 128
CHUNKS = 2
GROUPS = 2
PIECES = 3
MESH = pl.DeviceIdType.MESH
BF16 = jnp.bfloat16
F32 = jnp.float32


def dot(left, right, dims):
    return lax.dot_general(left, right, (dims, ((), ())), preferred_element_type=F32)


NN = ((1,), (0,))
NT = ((1,), (1,))
TN = ((0,), (0,))


def kernel(
    n, bits, heads, factor,
    x_hbm, q_hbm, k_hbm, v_hbm, g_hbm, ld_ref,
    gq_ref, gk_ref, gv_ref, ok_ref, ov_ref,
    q_ref, k_ref, v_ref, g_ref,
    cum_s, tot_s, kst_own, qst_own, kst, qst, tot_b, tot_a, w_b, w_a, pre, suf,
    acc_q, acc_k, acc_v, rx, rxt, gg, half_send, half_recv, lev_send, lev_recv,
    in_sem, st_send, st_recv, x_send, x_recv, xf_send, xf_recv, x_sem, g_send, g_recv,
    c_send, c_recv, l_send, l_recv, f_send, f_recv,
):
    s = lax.axis_index("seq")
    d = lax.axis_index("dp")
    head = lax.axis_index("head")
    length = q_ref.shape[0]
    cols = rx.shape[2]
    half = cols // 2
    size = half // CHUNKS
    piece = cols // PIECES
    group = heads // GROUPS
    parts = 2 * GROUPS
    wide = gg.shape[3]
    outs = (ok_ref, ov_ref)

    def partner(bit):
        block = 1 << bit
        low = lax.rem(lax.div(d, block), 2)
        return d + block - 2 * block * low

    near = partner(0)
    side = lax.rem(head, 2)
    mate = head + 1 - 2 * side
    loads = [
        pltpu.make_async_copy(src, dst, in_sem.at[i])
        for i, (src, dst) in enumerate(
            ((q_hbm, q_ref), (g_hbm, g_ref), (k_hbm, k_ref), (v_hbm, v_ref))
        )
    ]
    for copy in loads:
        copy.start()
    barrier = pltpu.get_barrier_semaphore()
    for step in range(1, n):
        pl.semaphore_signal(
            barrier, inc=1, device_id={"seq": lax.rem(s + step, n)}, device_id_type=MESH
        )
    for bit in range(bits):
        pl.semaphore_signal(barrier, inc=1, device_id={"dp": partner(bit)}, device_id_type=MESH)
    pl.semaphore_signal(barrier, inc=1, device_id={"head": mate}, device_id_type=MESH)
    x_own = pltpu.make_async_copy(
        x_hbm.at[:, pl.ds(pl.multiple_of(s * cols, 128), cols)], rx.at[0], x_sem
    )
    x_own.start()
    pl.semaphore_wait(barrier, n + bits)

    strip = pl.ds(pl.multiple_of(side * (length // 2), 16), length // 2)
    x_copies, x_swaps = {}, {}

    def x_start(i):
        for step in range(n - 1, 0, -1):
            peer = lax.rem(s + step, n)
            x_copies[i, step] = pltpu.make_async_remote_copy(
                src_ref=x_hbm.at[strip, pl.ds(pl.multiple_of(peer * cols + i * piece, 128), piece)],
                dst_ref=rx.at[step, strip, pl.ds(i * piece, piece)],
                send_sem=x_send.at[i, step - 1], recv_sem=x_recv.at[i, step - 1],
                device_id={"seq": peer}, device_id_type=MESH,
            )
            x_copies[i, step].start()

    def x_swap(i):
        for step in range(1, n):
            x_copies[i, step].wait_recv()
            here = rx.at[step, strip, pl.ds(i * piece, piece)]
            x_swaps[i, step] = pltpu.make_async_remote_copy(
                src_ref=here, dst_ref=here,
                send_sem=xf_send.at[i, step - 1], recv_sem=xf_recv.at[i, step - 1],
                device_id={"head": mate}, device_id_type=MESH,
            )
            x_swaps[i, step].start()

    def x_turn(i):
        for step in range(n):
            if step:
                x_swaps[i, step].wait_recv()
            rxt[i * piece : (i + 1) * piece, step * length : (step + 1) * length] = rx[
                step, :, i * piece : (i + 1) * piece
            ].T

    x_start(0)

    row = lax.broadcasted_iota(jnp.int32, (length, length), 0)
    col = lax.broadcasted_iota(jnp.int32, (length, length), 1)
    lower = row >= col
    tri = jnp.where(lower, 1.0, 0.0).astype(F32)
    tot_s[...] = jnp.zeros_like(tot_s)
    loads[0].wait()
    loads[1].wait()
    for h in range(heads):
        at = pl.ds(h * DH, DH)
        decays = jnp.broadcast_to(ld_ref[:, h : h + 1], (length, DH))
        cum = lax.dot_general(
            tri, decays, (NN, ((), ())), precision=lax.Precision.HIGHEST, preferred_element_type=F32
        )
        cum_s[h] = cum
        tot_s[h : h + 1, :] = cum[length - 1 : length, :]
        queries = (q_ref[:, at].astype(F32) * jnp.exp(cum)).astype(BF16)
        qst_own[h] = dot(queries, g_ref[:, at], TN).astype(BF16)

    def send(kind, step, src, dst, peer):
        return pltpu.make_async_remote_copy(
            src_ref=src, dst_ref=dst, send_sem=st_send.at[kind, step - 1],
            recv_sem=st_recv.at[kind, step - 1], device_id={"seq": peer}, device_id_type=MESH,
        )

    def forward(step):
        peer = lax.rem(s + step, n)
        return (
            send(0, step, tot_s, tot_b.at[step - 1], peer),
            send(1, step, kst_own, kst.at[step - 1], peer),
        )

    def backward(step):
        peer = lax.rem(s + n - step, n)
        return (
            send(2, step, tot_s, tot_a.at[step - 1], peer),
            send(3, step, qst_own, qst.at[step - 1], peer),
        )

    for step in range(n - 1, 0, -1):
        @pl.when(s >= step)
        def _(step=step):
            for copy in backward(step):
                copy.start()

    loads[2].wait()
    loads[3].wait()
    for h in range(heads):
        at = pl.ds(h * DH, DH)
        cum = cum_s[h]
        to_end = jnp.exp(cum[length - 1 : length, :] - cum)
        keys = (k_ref[:, at].astype(F32) * to_end).astype(BF16)
        kst_own[h] = dot(keys, v_ref[:, at], TN).astype(BF16)
    for i in range(1, PIECES):
        x_start(i)
    for step in range(n - 1, 0, -1):
        @pl.when(s + step < n)
        def _(step=step):
            for copy in forward(step):
                copy.start()

    for h in range(heads):
        at = pl.ds(h * DH, DH)
        cum = cum_s[h]
        mask = jnp.where(lower, jnp.exp(jnp.minimum(cum - cum.T, 0.0)), 0.0)
        q, k, v, g = q_ref[:, at], k_ref[:, at], v_ref[:, at], g_ref[:, at]
        value_weights = (dot(g, v, NT) * mask).astype(BF16)
        key_weights = (dot(q, k, NT) * mask).astype(BF16)
        acc_q[:, at] = dot(value_weights, k, NN)
        acc_k[:, at] = dot(value_weights, q, TN)
        acc_v[:, at] = dot(key_weights, g, TN)

    x_swap(0)

    for ref in (pre, suf, w_b, w_a):
        ref[...] = jnp.zeros_like(ref)
    for step in range(1, n):
        @pl.when(s + step < n)
        def _(step=step):
            for copy in backward(step):
                copy.wait_recv()
            weight = jnp.exp(w_a[...])
            for h in range(heads):
                suf[h] += weight[h : h + 1, :] * qst[step - 1, h].astype(F32)
            w_a[...] += tot_a[step - 1]

    scale = 1.0 / DH

    def relay(way, part, hop):
        step = 1 if way == 0 else n - 1
        have = hop if way == 0 else (n - hop) % n
        give = hop + 1 if way == 0 else n - hop - 1
        return pltpu.make_async_remote_copy(
            src_ref=gg.at[part, have], dst_ref=gg.at[part, give],
            send_sem=g_send.at[way, part, hop], recv_sem=g_recv.at[way, part, hop],
            device_id={"seq": lax.rem(s + step, n)}, device_id_type=MESH,
        )

    def sends(way, hop):
        if way == 0:
            return jnp.logical_and(s >= hop, s + 1 < n)
        return jnp.logical_and(s + hop < n, s >= 1)

    def gets(way, hop):
        return s >= hop + 1 if way == 0 else s + hop + 1 < n

    def pass_on(part, hop):
        for way in range(2):
            @pl.when(gets(way, hop))
            def _(way=way):
                relay(way, part, hop).wait_recv()

            if hop + 1 < n - 1:
                @pl.when(sends(way, hop + 1))
                def _(way=way):
                    relay(way, part, hop + 1).start()

    for part in range(parts):
        for i in range(group):
            h = (part % GROUPS) * group + i
            at = pl.ds(h * DH, DH)
            cum = cum_s[h]
            to_end = jnp.exp(cum[length - 1 : length, :] - cum)
            low_suffix = suf[h].astype(BF16)
            if part < GROUPS:
                carried = to_end * dot(v_ref[:, at], low_suffix, NT)
                result = ((acc_k[:, at] + carried) * scale).astype(BF16)
                gk_ref[:, at] = result
            else:
                carried = to_end * dot(k_ref[:, at], low_suffix, NN)
                result = ((acc_v[:, at] + carried) * scale).astype(BF16)
                gv_ref[:, at] = result
            gg[part, 0, :, i * DH : (i + 1) * DH] = result
        for way in range(2):
            @pl.when(sends(way, 0))
            def _(way=way, part=part):
                relay(way, part, 0).start()

    low = lax.rem(d, 2)
    own_row = low * half
    far_row = (1 - low) * half

    def product(start, part):
        rows = rxt[pl.ds(pl.multiple_of(start, 16), size), :]
        return dot(rows, gg[part].reshape(n * length, wide), NN)

    def exchange(src, dst, send_sem, recv_sem, to):
        return pltpu.make_async_remote_copy(
            src_ref=src, dst_ref=dst, send_sem=send_sem, recv_sem=recv_sem,
            device_id={"dp": to}, device_id_type=MESH,
        )

    def level_up(level, part, i):
        levels[level, part, i] = exchange(
            lev_send.at[level, part, i], lev_recv.at[level, part, i],
            l_send.at[level, part, i], l_recv.at[level, part, i], partner(level + 1),
        )
        levels[level, part, i].start()

    halves, levels, finals = {}, {}, {}

    def multiply(part):
        for i in range(CHUNKS):
            half_send[part, i] = product(far_row + i * size, part).astype(BF16)
            halves[part, i] = exchange(
                half_send.at[part, i], half_recv.at[part, i],
                c_send.at[part, i], c_recv.at[part, i], near,
            )
            halves[part, i].start()
        for i in range(CHUNKS):
            total = product(own_row + i * size, part)
            halves[part, i].wait_recv()
            total = total + half_recv[part, i].astype(F32)
            lev_send[0, part, i] = total.astype(BF16)
            level_up(0, part, i)

    pass_on(0, 0)
    for i in range(1, PIECES):
        x_swap(i)
    x_own.wait()
    x_turn(0)
    for wave in range(1, parts + n - 2):
        for part in range(parts):
            if 0 <= wave - part < n - 1:
                pass_on(part, wave - part)
        if wave <= n - 2:
            for i in range(1, PIECES):
                if (i - 1) * (n - 2) // (PIECES - 1) == wave - 1:
                    x_turn(i)
        if wave >= n - 2:
            multiply(wave - (n - 2))

    for step in range(1, n):
        @pl.when(s >= step)
        def _(step=step):
            for copy in forward(step):
                copy.wait_recv()
            weight = jnp.exp(w_b[...])
            for h in range(heads):
                pre[h] += weight[h : h + 1, :] * kst[step - 1, h].astype(F32)
            w_b[...] += tot_b[step - 1]
    for h in range(heads):
        at = pl.ds(h * DH, DH)
        carried = jnp.exp(cum_s[h]) * dot(g_ref[:, at], pre[h].astype(BF16), NT)
        gq_ref[:, at] = ((acc_q[:, at] + carried) * scale).astype(BF16)

    for level in range(bits - 1):
        for part in range(parts):
            for i in range(CHUNKS):
                levels[level, part, i].wait_recv()
                total = lev_send[level, part, i].astype(F32) + lev_recv[level, part, i].astype(F32)
                if level < bits - 2:
                    lev_send[level + 1, part, i] = total.astype(BF16)
                    level_up(level + 1, part, i)
                    continue
                here = outs[part // GROUPS].at[
                    pl.ds(pl.multiple_of(own_row + i * size, 16), size),
                    pl.ds((part % GROUPS) * wide, wide),
                ]
                here[...] = (total * factor).astype(BF16)
                finals[part, i] = exchange(
                    here, here, f_send.at[part, i], f_recv.at[part, i], near
                )
                finals[part, i].start()

    for step in range(1, n):
        @pl.when(s + step < n)
        def _(step=step):
            for copy in forward(step):
                copy.wait_send()

        @pl.when(s >= step)
        def _(step=step):
            for copy in backward(step):
                copy.wait_send()
    for hop in range(n - 1):
        for way in range(2):
            @pl.when(sends(way, hop))
            def _(way=way, hop=hop):
                for part in range(parts):
                    relay(way, part, hop).wait_send()
    for copies in (x_copies, x_swaps, halves, levels):
        for copy in copies.values():
            copy.wait_send()
    for copy in finals.values():
        copy.wait()


def per_device(layer_input, queries, key_rows, value_rows, grad_out, log_decay):
    n = lax.axis_size("seq")
    dp = lax.axis_size("dp")
    bits = dp.bit_length() - 1
    length, width = queries.shape[1:]
    heads = log_decay.shape[2]
    features = layer_input.shape[2]
    cols = features // n
    size = cols // 2 // CHUNKS
    parts = 2 * GROUPS
    wide = width // GROUPS
    tot_rows = -(-heads // 8) * 8
    factor = 1.0 / math.sqrt(dp * n * length)
    vmem = pl.BlockSpec(memory_space=pltpu.VMEM)
    dma = pltpu.SemaphoreType.DMA
    tile = (heads, DH, DH)
    grads = pl.pallas_call(
        functools.partial(kernel, n, bits, heads, factor),
        out_shape=[jax.ShapeDtypeStruct((length, width), BF16)] * 3
        + [jax.ShapeDtypeStruct((cols, width), BF16)] * 2,
        in_specs=[pl.BlockSpec(memory_space=pltpu.HBM)] * 5 + [vmem],
        out_specs=[vmem] * 5,
        scratch_shapes=[pltpu.VMEM((length, width), BF16)] * 4
        + [
            pltpu.VMEM((heads, length, DH), F32),
            pltpu.VMEM((tot_rows, DH), F32),
            pltpu.VMEM(tile, BF16),
            pltpu.VMEM(tile, BF16),
            pltpu.VMEM((n - 1,) + tile, BF16),
            pltpu.VMEM((n - 1,) + tile, BF16),
            pltpu.VMEM((n - 1, tot_rows, DH), F32),
            pltpu.VMEM((n - 1, tot_rows, DH), F32),
            pltpu.VMEM((tot_rows, DH), F32),
            pltpu.VMEM((tot_rows, DH), F32),
            pltpu.VMEM(tile, F32),
            pltpu.VMEM(tile, F32),
            pltpu.VMEM((length, width), F32),
            pltpu.VMEM((length, width), F32),
            pltpu.VMEM((length, width), F32),
            pltpu.VMEM((n, length, cols), BF16),
            pltpu.VMEM((cols, n * length), BF16),
            pltpu.VMEM((parts, n, length, wide), BF16),
            pltpu.VMEM((parts, CHUNKS, size, wide), BF16),
            pltpu.VMEM((parts, CHUNKS, size, wide), BF16),
            pltpu.VMEM((bits - 1, parts, CHUNKS, size, wide), BF16),
            pltpu.VMEM((bits - 1, parts, CHUNKS, size, wide), BF16),
            dma((4,)), dma((4, n - 1)), dma((4, n - 1)),
            dma((PIECES, n - 1)), dma((PIECES, n - 1)),
            dma((PIECES, n - 1)), dma((PIECES, n - 1)), dma,
            dma((2, parts, n - 1)), dma((2, parts, n - 1)),
            dma((parts, CHUNKS)), dma((parts, CHUNKS)),
            dma((bits - 1, parts, CHUNKS)), dma((bits - 1, parts, CHUNKS)),
            dma((parts, CHUNKS)), dma((parts, CHUNKS)),
        ],
        compiler_params=pltpu.CompilerParams(
            collective_id=0, has_side_effects=True, vmem_limit_bytes=48 << 20
        ),
    )(layer_input[0], queries[0], key_rows[0], value_rows[0], grad_out[0], log_decay[0])
    return (grads[0][None], grads[1][None], grads[2][None], grads[3], grads[4])


def solution(mesh):
    return jax.shard_map(
        per_device,
        mesh=mesh,
        in_specs=(
            P("dp", "seq", None),
            P("dp", "seq", "head"),
            P("dp", "seq", "head"),
            P("dp", "seq", "head"),
            P("dp", "seq", "head"),
            P("dp", "seq", "head"),
        ),
        out_specs=(
            P("dp", "seq", "head"),
            P("dp", "seq", "head"),
            P("dp", "seq", "head"),
            P("seq", "head"),
            P("seq", "head"),
        ),
        check_vma=False,
    )
```

```python
import functools
import math

import jax
import jax.numpy as jnp
from jax import lax
from jax.experimental import pallas as pl
from jax.experimental.pallas import tpu as pltpu
from jax.sharding import PartitionSpec as P

DH = 128
GROUPS = 2
PIECES = 3
MESH = pl.DeviceIdType.MESH
BF16 = jnp.bfloat16
F32 = jnp.float32


def dot(left, right, dims):
    return lax.dot_general(left, right, (dims, ((), ())), preferred_element_type=F32)


NN = ((1,), (0,))
NT = ((1,), (1,))
TN = ((0,), (0,))


def kernel(
    n, bits, heads, factor,
    x_hbm, q_hbm, k_hbm, v_hbm, g_hbm, ld_ref,
    gq_hbm, gk_hbm, gv_hbm, ok_hbm, ov_hbm,
    gq_ref, gk_ref, gv_ref, done,
    q_ref, k_ref, v_ref, g_ref,
    cum_s, tot_s, kst_own, qst_own, kst, qst, tot_b, tot_a, w_b, w_a, pre, suf,
    acc_q, acc_k, acc_v, rx, rxt, gg, half_send, half_recv, lev_send, lev_recv,
    in_sem, st_send, st_recv, x_send, x_recv, xf_send, xf_recv, x_sem, g_send, g_recv,
    c_send, c_recv, l_send, l_recv, f_send, f_recv, o_sem, small_sem,
):
    s = lax.axis_index("seq")
    d = lax.axis_index("dp")
    head = lax.axis_index("head")
    length = q_ref.shape[0]
    cols = rx.shape[2]
    piece = cols // PIECES
    size = piece // 2
    group = heads // GROUPS
    parts = 2 * GROUPS
    wide = gg.shape[3]
    outs = (ok_hbm, ov_hbm)

    def partner(bit):
        block = 1 << bit
        low = lax.rem(lax.div(d, block), 2)
        return d + block - 2 * block * low

    near = partner(0)
    side = lax.rem(head, 2)
    mate = head + 1 - 2 * side
    loads = [
        pltpu.make_async_copy(src, dst, in_sem.at[i])
        for i, (src, dst) in enumerate(
            ((q_hbm, q_ref), (g_hbm, g_ref), (k_hbm, k_ref), (v_hbm, v_ref))
        )
    ]
    for copy in loads:
        copy.start()
    barrier = pltpu.get_barrier_semaphore()
    for step in range(1, n):
        pl.semaphore_signal(
            barrier, inc=1, device_id={"seq": lax.rem(s + step, n)}, device_id_type=MESH
        )
    for bit in range(bits):
        pl.semaphore_signal(barrier, inc=1, device_id={"dp": partner(bit)}, device_id_type=MESH)
    pl.semaphore_signal(barrier, inc=1, device_id={"head": mate}, device_id_type=MESH)
    x_own = pltpu.make_async_copy(
        x_hbm.at[:, pl.ds(pl.multiple_of(s * cols, 128), cols)], rx.at[0], x_sem
    )
    x_own.start()
    pl.semaphore_wait(barrier, n + bits)

    strip = pl.ds(pl.multiple_of(side * (length // 2), 16), length // 2)
    x_copies, x_swaps = {}, {}

    def x_start(i):
        for step in range(n - 1, 0, -1):
            peer = lax.rem(s + step, n)
            x_copies[i, step] = pltpu.make_async_remote_copy(
                src_ref=x_hbm.at[strip, pl.ds(pl.multiple_of(peer * cols + i * piece, 128), piece)],
                dst_ref=rx.at[step, strip, pl.ds(i * piece, piece)],
                send_sem=x_send.at[i, step - 1], recv_sem=x_recv.at[i, step - 1],
                device_id={"seq": peer}, device_id_type=MESH,
            )
            x_copies[i, step].start()

    def x_swap(i):
        for step in range(1, n):
            x_copies[i, step].wait_recv()
            here = rx.at[step, strip, pl.ds(i * piece, piece)]
            x_swaps[i, step] = pltpu.make_async_remote_copy(
                src_ref=here, dst_ref=here,
                send_sem=xf_send.at[i, step - 1], recv_sem=xf_recv.at[i, step - 1],
                device_id={"head": mate}, device_id_type=MESH,
            )
            x_swaps[i, step].start()

    def x_turn(i):
        for step in range(n):
            if step:
                x_swaps[i, step].wait_recv()
            rxt[i * piece : (i + 1) * piece, step * length : (step + 1) * length] = rx[
                step, :, i * piece : (i + 1) * piece
            ].T

    x_start(0)

    row = lax.broadcasted_iota(jnp.int32, (length, length), 0)
    col = lax.broadcasted_iota(jnp.int32, (length, length), 1)
    lower = row >= col
    tri = jnp.where(lower, 1.0, 0.0).astype(F32)
    tot_s[...] = jnp.zeros_like(tot_s)
    loads[0].wait()
    loads[1].wait()
    for h in range(heads):
        at = pl.ds(h * DH, DH)
        decays = jnp.broadcast_to(ld_ref[:, h : h + 1], (length, DH))
        cum = lax.dot_general(
            tri, decays, (NN, ((), ())), precision=lax.Precision.HIGHEST, preferred_element_type=F32
        )
        cum_s[h] = cum
        tot_s[h : h + 1, :] = cum[length - 1 : length, :]
        queries = (q_ref[:, at].astype(F32) * jnp.exp(cum)).astype(BF16)
        qst_own[h] = dot(queries, g_ref[:, at], TN).astype(BF16)

    def send(kind, step, src, dst, peer):
        return pltpu.make_async_remote_copy(
            src_ref=src, dst_ref=dst, send_sem=st_send.at[kind, step - 1],
            recv_sem=st_recv.at[kind, step - 1], device_id={"seq": peer}, device_id_type=MESH,
        )

    def forward(step):
        peer = lax.rem(s + step, n)
        return (
            send(0, step, tot_s, tot_b.at[step - 1], peer),
            send(1, step, kst_own, kst.at[step - 1], peer),
        )

    def backward(step):
        peer = lax.rem(s + n - step, n)
        return (
            send(2, step, tot_s, tot_a.at[step - 1], peer),
            send(3, step, qst_own, qst.at[step - 1], peer),
        )

    for step in range(n - 1, 0, -1):
        @pl.when(s >= step)
        def _(step=step):
            for copy in backward(step):
                copy.start()

    loads[2].wait()
    loads[3].wait()
    for h in range(heads):
        at = pl.ds(h * DH, DH)
        cum = cum_s[h]
        to_end = jnp.exp(cum[length - 1 : length, :] - cum)
        keys = (k_ref[:, at].astype(F32) * to_end).astype(BF16)
        kst_own[h] = dot(keys, v_ref[:, at], TN).astype(BF16)

    for h in range(heads):
        at = pl.ds(h * DH, DH)
        cum = cum_s[h]
        mask = jnp.where(lower, jnp.exp(jnp.minimum(cum - cum.T, 0.0)), 0.0)
        q, k, v, g = q_ref[:, at], k_ref[:, at], v_ref[:, at], g_ref[:, at]
        value_weights = (dot(g, v, NT) * mask).astype(BF16)
        key_weights = (dot(q, k, NT) * mask).astype(BF16)
        acc_q[:, at] = dot(value_weights, k, NN)
        acc_k[:, at] = dot(value_weights, q, TN)
        acc_v[:, at] = dot(key_weights, g, TN)

    x_swap(0)

    for ref in (pre, suf, w_b, w_a):
        ref[...] = jnp.zeros_like(ref)
    for step in range(1, n):
        @pl.when(s + step < n)
        def _(step=step):
            for copy in backward(step):
                copy.wait_recv()
            weight = jnp.exp(w_a[...])
            for h in range(heads):
                suf[h] += weight[h : h + 1, :] * qst[step - 1, h].astype(F32)
            w_a[...] += tot_a[step - 1]

    scale = 1.0 / DH

    def relay(way, part, hop):
        step = 1 if way == 0 else n - 1
        have = hop if way == 0 else (n - hop) % n
        give = hop + 1 if way == 0 else n - hop - 1
        return pltpu.make_async_remote_copy(
            src_ref=gg.at[part, have], dst_ref=gg.at[part, give],
            send_sem=g_send.at[way, part, hop], recv_sem=g_recv.at[way, part, hop],
            device_id={"seq": lax.rem(s + step, n)}, device_id_type=MESH,
        )

    def sends(way, hop):
        if way == 0:
            return jnp.logical_and(s >= hop, s + 1 < n)
        return jnp.logical_and(s + hop < n, s >= 1)

    def gets(way, hop):
        return s >= hop + 1 if way == 0 else s + hop + 1 < n

    def pass_on(part, hop):
        for way in range(2):
            @pl.when(gets(way, hop))
            def _(way=way):
                relay(way, part, hop).wait_recv()

            if hop + 1 < n - 1:
                @pl.when(sends(way, hop + 1))
                def _(way=way):
                    relay(way, part, hop + 1).start()

    for part in range(parts):
        for i in range(group):
            h = (part % GROUPS) * group + i
            at = pl.ds(h * DH, DH)
            cum = cum_s[h]
            to_end = jnp.exp(cum[length - 1 : length, :] - cum)
            low_suffix = suf[h].astype(BF16)
            if part < GROUPS:
                carried = to_end * dot(v_ref[:, at], low_suffix, NT)
                result = ((acc_k[:, at] + carried) * scale).astype(BF16)
                gk_ref[:, at] = result
            else:
                carried = to_end * dot(k_ref[:, at], low_suffix, NN)
                result = ((acc_v[:, at] + carried) * scale).astype(BF16)
                gv_ref[:, at] = result
            gg[part, 0, :, i * DH : (i + 1) * DH] = result
        for way in range(2):
            @pl.when(sends(way, 0))
            def _(way=way, part=part):
                relay(way, part, 0).start()

    for i in range(1, PIECES):
        x_start(i)
    for step in range(n - 1, 0, -1):
        @pl.when(s + step < n)
        def _(step=step):
            for copy in forward(step):
                copy.start()
    writes = [
        pltpu.make_async_copy(src, dst, small_sem.at[i])
        for i, (src, dst) in enumerate(((gk_ref, gk_hbm), (gv_ref, gv_hbm), (gq_ref, gq_hbm)))
    ]
    writes[0].start()
    writes[1].start()

    low = lax.rem(d, 2)
    own_row = low * size
    far_row = (1 - low) * size

    def product(start, part):
        rows = rxt[pl.ds(pl.multiple_of(start, 16), size), :]
        return dot(rows, gg[part].reshape(n * length, wide), NN)

    def exchange(src, dst, send_sem, recv_sem, to):
        return pltpu.make_async_remote_copy(
            src_ref=src, dst_ref=dst, send_sem=send_sem, recv_sem=recv_sem,
            device_id={"dp": to}, device_id_type=MESH,
        )

    def level_up(level, part, i):
        levels[level, part, i] = exchange(
            lev_send.at[level, part, i], lev_recv.at[level, part, i],
            l_send.at[level, part, i], l_recv.at[level, part, i], partner(level + 1),
        )
        levels[level, part, i].start()

    halves, levels, finals = {}, {}, {}

    def multiply(i, part):
        half_send[part, i] = product(far_row + i * piece, part).astype(BF16)
        halves[part, i] = exchange(
            half_send.at[part, i], half_recv.at[part, i],
            c_send.at[part, i], c_recv.at[part, i], near,
        )
        halves[part, i].start()
        total = product(own_row + i * piece, part)
        halves[part, i].wait_recv()
        total = total + half_recv[part, i].astype(F32)
        lev_send[0, part, i] = total.astype(BF16)
        level_up(0, part, i)

    pass_on(0, 0)
    x_own.wait()
    x_turn(0)
    for wave in range(1, parts + n - 2):
        for part in range(parts):
            if 0 <= wave - part < n - 1:
                pass_on(part, wave - part)
        if wave >= n - 2:
            multiply(0, wave - (n - 2))
    for i in range(1, PIECES):
        x_swap(i)
        x_turn(i)
        for part in range(parts):
            multiply(i, part)

    for step in range(1, n):
        @pl.when(s >= step)
        def _(step=step):
            for copy in forward(step):
                copy.wait_recv()
            weight = jnp.exp(w_b[...])
            for h in range(heads):
                pre[h] += weight[h : h + 1, :] * kst[step - 1, h].astype(F32)
            w_b[...] += tot_b[step - 1]
    for h in range(heads):
        at = pl.ds(h * DH, DH)
        carried = jnp.exp(cum_s[h]) * dot(g_ref[:, at], pre[h].astype(BF16), NT)
        gq_ref[:, at] = ((acc_q[:, at] + carried) * scale).astype(BF16)
    writes[2].start()

    for level in range(bits - 1):
        for i in range(PIECES):
            for part in range(parts):
                levels[level, part, i].wait_recv()
                total = lev_send[level, part, i].astype(F32) + lev_recv[level, part, i].astype(F32)
                if level < bits - 2:
                    lev_send[level + 1, part, i] = total.astype(BF16)
                    level_up(level + 1, part, i)
                    continue
                here = outs[part // GROUPS].at[
                    pl.ds(pl.multiple_of(own_row + i * piece, 16), size),
                    pl.ds((part % GROUPS) * wide, wide),
                ]
                done[part, i] = (total * factor).astype(BF16)
                copy = pltpu.make_async_copy(done.at[part, i], here, o_sem.at[part, i])
                copy.start()
                writes.append(copy)
                finals[part, i] = exchange(
                    done.at[part, i], here, f_send.at[part, i], f_recv.at[part, i], near
                )
                finals[part, i].start()

    for step in range(1, n):
        @pl.when(s + step < n)
        def _(step=step):
            for copy in forward(step):
                copy.wait_send()

        @pl.when(s >= step)
        def _(step=step):
            for copy in backward(step):
                copy.wait_send()
    for hop in range(n - 1):
        for way in range(2):
            @pl.when(sends(way, hop))
            def _(way=way, hop=hop):
                for part in range(parts):
                    relay(way, part, hop).wait_send()
    for copies in (x_copies, x_swaps, halves, levels):
        for copy in copies.values():
            copy.wait_send()
    for copy in list(finals.values()) + writes:
        copy.wait()


def emit(*refs):
    sems = refs[-1]
    copies = [pltpu.make_async_copy(refs[i], refs[5 + i], sems.at[i]) for i in range(5)]
    for copy in copies:
        copy.start()
    for copy in copies:
        copy.wait()


def per_device(layer_input, queries, key_rows, value_rows, grad_out, log_decay):
    n = lax.axis_size("seq")
    dp = lax.axis_size("dp")
    bits = dp.bit_length() - 1
    length, width = queries.shape[1:]
    heads = log_decay.shape[2]
    features = layer_input.shape[2]
    cols = features // n
    size = cols // PIECES // 2
    parts = 2 * GROUPS
    wide = width // GROUPS
    tot_rows = -(-heads // 8) * 8
    factor = 1.0 / math.sqrt(dp * n * length)
    vmem = pl.BlockSpec(memory_space=pltpu.VMEM)
    dma = pltpu.SemaphoreType.DMA
    tile = (heads, DH, DH)
    grads = pl.pallas_call(
        functools.partial(kernel, n, bits, heads, factor),
        out_shape=[jax.ShapeDtypeStruct((length, width), BF16)] * 3
        + [jax.ShapeDtypeStruct((cols, width), BF16)] * 2,
        in_specs=[pl.BlockSpec(memory_space=pltpu.HBM)] * 5 + [vmem],
        out_specs=[pl.BlockSpec(memory_space=pltpu.HBM)] * 5,
        scratch_shapes=[pltpu.VMEM((length, width), BF16)] * 3
        + [pltpu.VMEM((parts, PIECES, size, wide), BF16)]
        + [pltpu.VMEM((length, width), BF16)] * 4
        + [
            pltpu.VMEM((heads, length, DH), F32),
            pltpu.VMEM((tot_rows, DH), F32),
            pltpu.VMEM(tile, BF16),
            pltpu.VMEM(tile, BF16),
            pltpu.VMEM((n - 1,) + tile, BF16),
            pltpu.VMEM((n - 1,) + tile, BF16),
            pltpu.VMEM((n - 1, tot_rows, DH), F32),
            pltpu.VMEM((n - 1, tot_rows, DH), F32),
            pltpu.VMEM((tot_rows, DH), F32),
            pltpu.VMEM((tot_rows, DH), F32),
            pltpu.VMEM(tile, F32),
            pltpu.VMEM(tile, F32),
            pltpu.VMEM((length, width), F32),
            pltpu.VMEM((length, width), F32),
            pltpu.VMEM((length, width), F32),
            pltpu.VMEM((n, length, cols), BF16),
            pltpu.VMEM((cols, n * length), BF16),
            pltpu.VMEM((parts, n, length, wide), BF16),
            pltpu.VMEM((parts, PIECES, size, wide), BF16),
            pltpu.VMEM((parts, PIECES, size, wide), BF16),
            pltpu.VMEM((bits - 1, parts, PIECES, size, wide), BF16),
            pltpu.VMEM((bits - 1, parts, PIECES, size, wide), BF16),
            dma((4,)), dma((4, n - 1)), dma((4, n - 1)),
            dma((PIECES, n - 1)), dma((PIECES, n - 1)),
            dma((PIECES, n - 1)), dma((PIECES, n - 1)), dma,
            dma((2, parts, n - 1)), dma((2, parts, n - 1)),
            dma((parts, PIECES)), dma((parts, PIECES)),
            dma((bits - 1, parts, PIECES)), dma((bits - 1, parts, PIECES)),
            dma((parts, PIECES)), dma((parts, PIECES)),
            dma((parts, PIECES)), dma((3,)),
        ],
        compiler_params=pltpu.CompilerParams(
            collective_id=0, has_side_effects=True, vmem_limit_bytes=60 << 20
        ),
    )(layer_input[0], queries[0], key_rows[0], value_rows[0], grad_out[0], log_decay[0])
    hbm = pl.BlockSpec(memory_space=pltpu.HBM)
    grads = pl.pallas_call(
        emit,
        out_shape=[jax.ShapeDtypeStruct(a.shape, a.dtype) for a in grads],
        in_specs=[hbm] * 5,
        out_specs=[hbm] * 5,
        scratch_shapes=[dma((5,))],
    )(*grads)
    return (grads[0][None], grads[1][None], grads[2][None], grads[3], grads[4])


def solution(mesh):
    return jax.shard_map(
        per_device,
        mesh=mesh,
        in_specs=(
            P("dp", "seq", None),
            P("dp", "seq", "head"),
            P("dp", "seq", "head"),
            P("dp", "seq", "head"),
            P("dp", "seq", "head"),
            P("dp", "seq", "head"),
        ),
        out_specs=(
            P("dp", "seq", "head"),
            P("dp", "seq", "head"),
            P("dp", "seq", "head"),
            P("seq", "head"),
            P("seq", "head"),
        ),
        check_vma=False,
    )
```

```python
import functools
import math

import jax
import jax.numpy as jnp
from jax import lax
from jax.experimental import pallas as pl
from jax.experimental.pallas import tpu as pltpu
from jax.sharding import PartitionSpec as P

DH = 128
GROUPS = 2
PIECES = 3
MESH = pl.DeviceIdType.MESH
BF16 = jnp.bfloat16
F32 = jnp.float32


def dot(left, right, dims):
    return lax.dot_general(left, right, (dims, ((), ())), preferred_element_type=F32)


NN = ((1,), (0,))
NT = ((1,), (1,))
TN = ((0,), (0,))


def kernel(
    n, bits, heads, factor,
    x_hbm, q_hbm, k_hbm, v_hbm, g_hbm, ld_ref,
    gq_ref, gk_ref, gv_ref, ok_ref, ov_ref,
    q_ref, k_ref, v_ref, g_ref,
    cum_s, tot_s, kst_own, qst_own, kst, qst, tot_b, tot_a, w_b, w_a, pre, suf,
    acc_q, acc_k, acc_v, rx, rxt, gg, half_send, half_recv, lev_send, lev_recv,
    in_sem, st_send, st_recv, x_send, x_recv, xf_send, xf_recv, x_sem, g_send, g_recv,
    c_send, c_recv, l_send, l_recv, f_send, f_recv,
):
    s = lax.axis_index("seq")
    d = lax.axis_index("dp")
    head = lax.axis_index("head")
    length = q_ref.shape[0]
    cols = rx.shape[2]
    piece = cols // PIECES
    size = piece // 2
    group = heads // GROUPS
    parts = 2 * GROUPS
    wide = gg.shape[3]
    outs = (ok_ref, ov_ref)

    def partner(bit):
        block = 1 << bit
        low = lax.rem(lax.div(d, block), 2)
        return d + block - 2 * block * low

    near = partner(0)
    side = lax.rem(head, 2)
    mate = head + 1 - 2 * side
    loads = [
        pltpu.make_async_copy(src, dst, in_sem.at[i])
        for i, (src, dst) in enumerate(
            ((q_hbm, q_ref), (g_hbm, g_ref), (k_hbm, k_ref), (v_hbm, v_ref))
        )
    ]
    for copy in loads:
        copy.start()
    barrier = pltpu.get_barrier_semaphore()
    for step in range(1, n):
        pl.semaphore_signal(
            barrier, inc=1, device_id={"seq": lax.rem(s + step, n)}, device_id_type=MESH
        )
    for bit in range(bits):
        pl.semaphore_signal(barrier, inc=1, device_id={"dp": partner(bit)}, device_id_type=MESH)
    pl.semaphore_signal(barrier, inc=1, device_id={"head": mate}, device_id_type=MESH)
    x_own = pltpu.make_async_copy(
        x_hbm.at[:, pl.ds(pl.multiple_of(s * cols, 128), cols)], rx.at[0], x_sem
    )
    x_own.start()
    pl.semaphore_wait(barrier, n + bits)

    strip = pl.ds(pl.multiple_of(side * (length // 2), 16), length // 2)
    x_copies, x_swaps = {}, {}

    def x_start(i):
        for step in range(n - 1, 0, -1):
            peer = lax.rem(s + step, n)
            x_copies[i, step] = pltpu.make_async_remote_copy(
                src_ref=x_hbm.at[strip, pl.ds(pl.multiple_of(peer * cols + i * piece, 128), piece)],
                dst_ref=rx.at[step, strip, pl.ds(i * piece, piece)],
                send_sem=x_send.at[i, step - 1], recv_sem=x_recv.at[i, step - 1],
                device_id={"seq": peer}, device_id_type=MESH,
            )
            x_copies[i, step].start()

    def x_swap(i):
        for step in range(1, n):
            x_copies[i, step].wait_recv()
            here = rx.at[step, strip, pl.ds(i * piece, piece)]
            x_swaps[i, step] = pltpu.make_async_remote_copy(
                src_ref=here, dst_ref=here,
                send_sem=xf_send.at[i, step - 1], recv_sem=xf_recv.at[i, step - 1],
                device_id={"head": mate}, device_id_type=MESH,
            )
            x_swaps[i, step].start()

    def x_turn(i):
        for step in range(n):
            if step:
                x_swaps[i, step].wait_recv()
            rxt[i * piece : (i + 1) * piece, step * length : (step + 1) * length] = rx[
                step, :, i * piece : (i + 1) * piece
            ].T

    x_start(0)

    row = lax.broadcasted_iota(jnp.int32, (length, length), 0)
    col = lax.broadcasted_iota(jnp.int32, (length, length), 1)
    lower = row >= col
    tri = jnp.where(lower, 1.0, 0.0).astype(F32)
    tot_s[...] = jnp.zeros_like(tot_s)
    loads[0].wait()
    loads[1].wait()
    for h in range(heads):
        at = pl.ds(h * DH, DH)
        decays = jnp.broadcast_to(ld_ref[:, h : h + 1], (length, DH))
        cum = lax.dot_general(
            tri, decays, (NN, ((), ())), precision=lax.Precision.HIGHEST, preferred_element_type=F32
        )
        cum_s[h] = cum
        tot_s[h : h + 1, :] = cum[length - 1 : length, :]
        queries = (q_ref[:, at].astype(F32) * jnp.exp(cum)).astype(BF16)
        qst_own[h] = dot(queries, g_ref[:, at], TN).astype(BF16)

    def send(kind, step, src, dst, peer):
        return pltpu.make_async_remote_copy(
            src_ref=src, dst_ref=dst, send_sem=st_send.at[kind, step - 1],
            recv_sem=st_recv.at[kind, step - 1], device_id={"seq": peer}, device_id_type=MESH,
        )

    def forward(step):
        peer = lax.rem(s + step, n)
        return (
            send(0, step, tot_s, tot_b.at[step - 1], peer),
            send(1, step, kst_own, kst.at[step - 1], peer),
        )

    def backward(step):
        peer = lax.rem(s + n - step, n)
        return (
            send(2, step, tot_s, tot_a.at[step - 1], peer),
            send(3, step, qst_own, qst.at[step - 1], peer),
        )

    for step in range(n - 1, 0, -1):
        @pl.when(s >= step)
        def _(step=step):
            for copy in backward(step):
                copy.start()

    loads[2].wait()
    loads[3].wait()
    for h in range(heads):
        at = pl.ds(h * DH, DH)
        cum = cum_s[h]
        to_end = jnp.exp(cum[length - 1 : length, :] - cum)
        keys = (k_ref[:, at].astype(F32) * to_end).astype(BF16)
        kst_own[h] = dot(keys, v_ref[:, at], TN).astype(BF16)

    for h in range(heads):
        at = pl.ds(h * DH, DH)
        cum = cum_s[h]
        mask = jnp.where(lower, jnp.exp(jnp.minimum(cum - cum.T, 0.0)), 0.0)
        q, k, v, g = q_ref[:, at], k_ref[:, at], v_ref[:, at], g_ref[:, at]
        value_weights = (dot(g, v, NT) * mask).astype(BF16)
        key_weights = (dot(q, k, NT) * mask).astype(BF16)
        acc_q[:, at] = dot(value_weights, k, NN)
        acc_k[:, at] = dot(value_weights, q, TN)
        acc_v[:, at] = dot(key_weights, g, TN)

    x_swap(0)

    for ref in (pre, suf, w_b, w_a):
        ref[...] = jnp.zeros_like(ref)
    for step in range(1, n):
        @pl.when(s + step < n)
        def _(step=step):
            for copy in backward(step):
                copy.wait_recv()
            weight = jnp.exp(w_a[...])
            for h in range(heads):
                suf[h] += weight[h : h + 1, :] * qst[step - 1, h].astype(F32)
            w_a[...] += tot_a[step - 1]

    scale = 1.0 / DH

    def relay(way, part, hop):
        step = 1 if way == 0 else n - 1
        have = hop if way == 0 else (n - hop) % n
        give = hop + 1 if way == 0 else n - hop - 1
        return pltpu.make_async_remote_copy(
            src_ref=gg.at[part, have], dst_ref=gg.at[part, give],
            send_sem=g_send.at[way, part, hop], recv_sem=g_recv.at[way, part, hop],
            device_id={"seq": lax.rem(s + step, n)}, device_id_type=MESH,
        )

    def sends(way, hop):
        if way == 0:
            return jnp.logical_and(s >= hop, s + 1 < n)
        return jnp.logical_and(s + hop < n, s >= 1)

    def gets(way, hop):
        return s >= hop + 1 if way == 0 else s + hop + 1 < n

    def pass_on(part, hop):
        for way in range(2):
            @pl.when(gets(way, hop))
            def _(way=way):
                relay(way, part, hop).wait_recv()

            if hop + 1 < n - 1:
                @pl.when(sends(way, hop + 1))
                def _(way=way):
                    relay(way, part, hop + 1).start()

    for part in range(parts):
        for i in range(group):
            h = (part % GROUPS) * group + i
            at = pl.ds(h * DH, DH)
            cum = cum_s[h]
            to_end = jnp.exp(cum[length - 1 : length, :] - cum)
            low_suffix = suf[h].astype(BF16)
            if part < GROUPS:
                carried = to_end * dot(v_ref[:, at], low_suffix, NT)
                result = ((acc_k[:, at] + carried) * scale).astype(BF16)
                gk_ref[:, at] = result
            else:
                carried = to_end * dot(k_ref[:, at], low_suffix, NN)
                result = ((acc_v[:, at] + carried) * scale).astype(BF16)
                gv_ref[:, at] = result
            gg[part, 0, :, i * DH : (i + 1) * DH] = result
        for way in range(2):
            @pl.when(sends(way, 0))
            def _(way=way, part=part):
                relay(way, part, 0).start()

    for i in range(1, PIECES):
        x_start(i)
    for step in range(n - 1, 0, -1):
        @pl.when(s + step < n)
        def _(step=step):
            for copy in forward(step):
                copy.start()

    low = lax.rem(d, 2)
    own_row = low * size
    far_row = (1 - low) * size

    def product(start, part):
        rows = rxt[pl.ds(pl.multiple_of(start, 16), size), :]
        return dot(rows, gg[part].reshape(n * length, wide), NN)

    def exchange(src, dst, send_sem, recv_sem, to):
        return pltpu.make_async_remote_copy(
            src_ref=src, dst_ref=dst, send_sem=send_sem, recv_sem=recv_sem,
            device_id={"dp": to}, device_id_type=MESH,
        )

    def level_up(level, part, i):
        levels[level, part, i] = exchange(
            lev_send.at[level, part, i], lev_recv.at[level, part, i],
            l_send.at[level, part, i], l_recv.at[level, part, i], partner(level + 1),
        )
        levels[level, part, i].start()

    halves, levels, finals = {}, {}, {}

    def multiply(i, part):
        half_send[part, i] = product(far_row + i * piece, part).astype(BF16)
        halves[part, i] = exchange(
            half_send.at[part, i], half_recv.at[part, i],
            c_send.at[part, i], c_recv.at[part, i], near,
        )
        halves[part, i].start()
        total = product(own_row + i * piece, part)
        halves[part, i].wait_recv()
        total = total + half_recv[part, i].astype(F32)
        lev_send[0, part, i] = total.astype(BF16)
        level_up(0, part, i)

    pass_on(0, 0)
    x_own.wait()
    x_turn(0)
    for wave in range(1, parts + n - 2):
        for part in range(parts):
            if 0 <= wave - part < n - 1:
                pass_on(part, wave - part)
        if wave >= n - 2:
            multiply(0, wave - (n - 2))
    for i in range(1, PIECES):
        x_swap(i)
        x_turn(i)
        for part in range(parts):
            multiply(i, part)

    for step in range(1, n):
        @pl.when(s >= step)
        def _(step=step):
            for copy in forward(step):
                copy.wait_recv()
            weight = jnp.exp(w_b[...])
            for h in range(heads):
                pre[h] += weight[h : h + 1, :] * kst[step - 1, h].astype(F32)
            w_b[...] += tot_b[step - 1]
    for h in range(heads):
        at = pl.ds(h * DH, DH)
        carried = jnp.exp(cum_s[h]) * dot(g_ref[:, at], pre[h].astype(BF16), NT)
        gq_ref[:, at] = ((acc_q[:, at] + carried) * scale).astype(BF16)

    for level in range(bits - 1):
        for i in range(PIECES):
            for part in range(parts):
                levels[level, part, i].wait_recv()
                total = lev_send[level, part, i].astype(F32) + lev_recv[level, part, i].astype(F32)
                if level < bits - 2:
                    lev_send[level + 1, part, i] = total.astype(BF16)
                    level_up(level + 1, part, i)
                    continue
                here = outs[part // GROUPS].at[
                    pl.ds(pl.multiple_of(own_row + i * piece, 16), size),
                    pl.ds((part % GROUPS) * wide, wide),
                ]
                here[...] = (total * factor).astype(BF16)
                finals[part, i] = exchange(
                    here, here, f_send.at[part, i], f_recv.at[part, i], near
                )
                finals[part, i].start()

    for step in range(1, n):
        @pl.when(s + step < n)
        def _(step=step):
            for copy in forward(step):
                copy.wait_send()

        @pl.when(s >= step)
        def _(step=step):
            for copy in backward(step):
                copy.wait_send()
    for hop in range(n - 1):
        for way in range(2):
            @pl.when(sends(way, hop))
            def _(way=way, hop=hop):
                for part in range(parts):
                    relay(way, part, hop).wait_send()
    for copies in (x_copies, x_swaps, halves, levels):
        for copy in copies.values():
            copy.wait_send()
    for copy in finals.values():
        copy.wait()


def per_device(layer_input, queries, key_rows, value_rows, grad_out, log_decay):
    n = lax.axis_size("seq")
    dp = lax.axis_size("dp")
    bits = dp.bit_length() - 1
    length, width = queries.shape[1:]
    heads = log_decay.shape[2]
    features = layer_input.shape[2]
    cols = features // n
    size = cols // PIECES // 2
    parts = 2 * GROUPS
    wide = width // GROUPS
    tot_rows = -(-heads // 8) * 8
    factor = 1.0 / math.sqrt(dp * n * length)
    vmem = pl.BlockSpec(memory_space=pltpu.VMEM)
    dma = pltpu.SemaphoreType.DMA
    tile = (heads, DH, DH)
    grads = pl.pallas_call(
        functools.partial(kernel, n, bits, heads, factor),
        out_shape=[jax.ShapeDtypeStruct((length, width), BF16)] * 3
        + [jax.ShapeDtypeStruct((cols, width), BF16)] * 2,
        in_specs=[pl.BlockSpec(memory_space=pltpu.HBM)] * 5 + [vmem],
        out_specs=[vmem] * 5,
        scratch_shapes=[pltpu.VMEM((length, width), BF16)] * 4
        + [
            pltpu.VMEM((heads, length, DH), F32),
            pltpu.VMEM((tot_rows, DH), F32),
            pltpu.VMEM(tile, BF16),
            pltpu.VMEM(tile, BF16),
            pltpu.VMEM((n - 1,) + tile, BF16),
            pltpu.VMEM((n - 1,) + tile, BF16),
            pltpu.VMEM((n - 1, tot_rows, DH), F32),
            pltpu.VMEM((n - 1, tot_rows, DH), F32),
            pltpu.VMEM((tot_rows, DH), F32),
            pltpu.VMEM((tot_rows, DH), F32),
            pltpu.VMEM(tile, F32),
            pltpu.VMEM(tile, F32),
            pltpu.VMEM((length, width), F32),
            pltpu.VMEM((length, width), F32),
            pltpu.VMEM((length, width), F32),
            pltpu.VMEM((n, length, cols), BF16),
            pltpu.VMEM((cols, n * length), BF16),
            pltpu.VMEM((parts, n, length, wide), BF16),
            pltpu.VMEM((parts, PIECES, size, wide), BF16),
            pltpu.VMEM((parts, PIECES, size, wide), BF16),
            pltpu.VMEM((bits - 1, parts, PIECES, size, wide), BF16),
            pltpu.VMEM((bits - 1, parts, PIECES, size, wide), BF16),
            dma((4,)), dma((4, n - 1)), dma((4, n - 1)),
            dma((PIECES, n - 1)), dma((PIECES, n - 1)),
            dma((PIECES, n - 1)), dma((PIECES, n - 1)), dma,
            dma((2, parts, n - 1)), dma((2, parts, n - 1)),
            dma((parts, PIECES)), dma((parts, PIECES)),
            dma((bits - 1, parts, PIECES)), dma((bits - 1, parts, PIECES)),
            dma((parts, PIECES)), dma((parts, PIECES)),
        ],
        compiler_params=pltpu.CompilerParams(
            collective_id=0, has_side_effects=True, vmem_limit_bytes=48 << 20
        ),
    )(layer_input[0], queries[0], key_rows[0], value_rows[0], grad_out[0], log_decay[0])
    return (grads[0][None], grads[1][None], grads[2][None], grads[3], grads[4])


def solution(mesh):
    return jax.shard_map(
        per_device,
        mesh=mesh,
        in_specs=(
            P("dp", "seq", None),
            P("dp", "seq", "head"),
            P("dp", "seq", "head"),
            P("dp", "seq", "head"),
            P("dp", "seq", "head"),
            P("dp", "seq", "head"),
        ),
        out_specs=(
            P("dp", "seq", "head"),
            P("dp", "seq", "head"),
            P("dp", "seq", "head"),
            P("seq", "head"),
            P("seq", "head"),
        ),
        check_vma=False,
    )
```

```python
import functools
import math

import jax
import jax.numpy as jnp
from jax import lax
from jax.experimental import pallas as pl
from jax.experimental.pallas import tpu as pltpu
from jax.sharding import PartitionSpec as P

DH = 128
GROUPS = 2
PIECES = 3
MESH = pl.DeviceIdType.MESH
BF16 = jnp.bfloat16
F32 = jnp.float32


def dot(left, right, dims):
    return lax.dot_general(left, right, (dims, ((), ())), preferred_element_type=F32)


NN = ((1,), (0,))
NT = ((1,), (1,))
TN = ((0,), (0,))


def kernel(
    n, bits, heads, factor,
    x_hbm, q_hbm, k_hbm, v_hbm, g_hbm, ld_ref,
    gq_ref, gk_ref, gv_ref, ok_ref, ov_ref,
    q_ref, k_ref, v_ref, g_ref,
    cum_s, tot_s, kst_own, qst_own, kst, qst, tot_b, tot_a, w_b, w_a, pre, suf,
    acc_q, acc_k, acc_v, rx, rxt, gg, half_send, half_recv, lev_send, lev_recv,
    in_sem, st_send, st_recv, x_send, x_recv, xf_send, xf_recv, x_sem, g_send, g_recv,
    c_send, c_recv, l_send, l_recv, f_send, f_recv,
):
    s = lax.axis_index("seq")
    d = lax.axis_index("dp")
    head = lax.axis_index("head")
    length = q_ref.shape[0]
    cols = rx.shape[2]
    piece = cols // PIECES
    size = piece // 2
    group = heads // GROUPS
    parts = 2 * GROUPS
    wide = gg.shape[3]
    outs = (ok_ref, ov_ref)

    def partner(bit):
        block = 1 << bit
        low = lax.rem(lax.div(d, block), 2)
        return d + block - 2 * block * low

    near = partner(0)
    side = lax.rem(head, 2)
    mate = head + 1 - 2 * side
    loads = [
        pltpu.make_async_copy(src, dst, in_sem.at[i])
        for i, (src, dst) in enumerate(
            ((q_hbm, q_ref), (g_hbm, g_ref), (k_hbm, k_ref), (v_hbm, v_ref))
        )
    ]
    for copy in loads:
        copy.start()
    barrier = pltpu.get_barrier_semaphore()
    for step in range(1, n):
        pl.semaphore_signal(
            barrier, inc=1, device_id={"seq": lax.rem(s + step, n)}, device_id_type=MESH
        )
    for bit in range(bits):
        pl.semaphore_signal(barrier, inc=1, device_id={"dp": partner(bit)}, device_id_type=MESH)
    pl.semaphore_signal(barrier, inc=1, device_id={"head": mate}, device_id_type=MESH)
    x_own = pltpu.make_async_copy(
        x_hbm.at[:, pl.ds(pl.multiple_of(s * cols, 128), cols)], rx.at[0], x_sem
    )
    x_own.start()
    pl.semaphore_wait(barrier, n + bits)

    strip = pl.ds(pl.multiple_of(side * (length // 2), 16), length // 2)
    x_copies, x_swaps = {}, {}

    def x_start(i):
        for step in range(n - 1, 0, -1):
            peer = lax.rem(s + step, n)
            x_copies[i, step] = pltpu.make_async_remote_copy(
                src_ref=x_hbm.at[strip, pl.ds(pl.multiple_of(peer * cols + i * piece, 128), piece)],
                dst_ref=rx.at[step, strip, pl.ds(i * piece, piece)],
                send_sem=x_send.at[i, step - 1], recv_sem=x_recv.at[i, step - 1],
                device_id={"seq": peer}, device_id_type=MESH,
            )
            x_copies[i, step].start()

    def x_swap(i):
        for step in range(1, n):
            x_copies[i, step].wait_recv()
            here = rx.at[step, strip, pl.ds(i * piece, piece)]
            x_swaps[i, step] = pltpu.make_async_remote_copy(
                src_ref=here, dst_ref=here,
                send_sem=xf_send.at[i, step - 1], recv_sem=xf_recv.at[i, step - 1],
                device_id={"head": mate}, device_id_type=MESH,
            )
            x_swaps[i, step].start()

    def x_turn(i):
        for step in range(n):
            if step:
                x_swaps[i, step].wait_recv()
            rxt[i * piece : (i + 1) * piece, step * length : (step + 1) * length] = rx[
                step, :, i * piece : (i + 1) * piece
            ].T

    x_start(0)

    row = lax.broadcasted_iota(jnp.int32, (length, length), 0)
    col = lax.broadcasted_iota(jnp.int32, (length, length), 1)
    lower = row >= col
    tri = jnp.where(lower, 1.0, 0.0).astype(F32)
    tot_s[...] = jnp.zeros_like(tot_s)
    loads[0].wait()
    loads[1].wait()
    for h in range(heads):
        at = pl.ds(h * DH, DH)
        decays = jnp.broadcast_to(ld_ref[:, h : h + 1], (length, DH))
        cum = lax.dot_general(
            tri, decays, (NN, ((), ())), precision=lax.Precision.HIGHEST, preferred_element_type=F32
        )
        cum_s[h] = cum
        tot_s[h : h + 1, :] = cum[length - 1 : length, :]
        queries = (q_ref[:, at].astype(F32) * jnp.exp(cum)).astype(BF16)
        qst_own[h] = dot(queries, g_ref[:, at], TN).astype(BF16)

    def send(kind, step, src, dst, peer):
        return pltpu.make_async_remote_copy(
            src_ref=src, dst_ref=dst, send_sem=st_send.at[kind, step - 1],
            recv_sem=st_recv.at[kind, step - 1], device_id={"seq": peer}, device_id_type=MESH,
        )

    def forward(step):
        peer = lax.rem(s + step, n)
        return (
            send(0, step, tot_s, tot_b.at[step - 1], peer),
            send(1, step, kst_own, kst.at[step - 1], peer),
        )

    def backward(step):
        peer = lax.rem(s + n - step, n)
        return (
            send(2, step, tot_s, tot_a.at[step - 1], peer),
            send(3, step, qst_own, qst.at[step - 1], peer),
        )

    for step in range(n - 1, 0, -1):
        @pl.when(s >= step)
        def _(step=step):
            for copy in backward(step):
                copy.start()

    loads[2].wait()
    loads[3].wait()
    for h in range(heads):
        at = pl.ds(h * DH, DH)
        cum = cum_s[h]
        to_end = jnp.exp(cum[length - 1 : length, :] - cum)
        keys = (k_ref[:, at].astype(F32) * to_end).astype(BF16)
        kst_own[h] = dot(keys, v_ref[:, at], TN).astype(BF16)

    for i in range(1, PIECES):
        x_start(i)
    for step in range(n - 1, 0, -1):
        @pl.when(s + step < n)
        def _(step=step):
            for copy in forward(step):
                copy.start()

    for h in range(heads):
        at = pl.ds(h * DH, DH)
        cum = cum_s[h]
        mask = jnp.where(lower, jnp.exp(jnp.minimum(cum - cum.T, 0.0)), 0.0)
        q, k, v, g = q_ref[:, at], k_ref[:, at], v_ref[:, at], g_ref[:, at]
        value_weights = (dot(g, v, NT) * mask).astype(BF16)
        key_weights = (dot(q, k, NT) * mask).astype(BF16)
        acc_q[:, at] = dot(value_weights, k, NN)
        acc_k[:, at] = dot(value_weights, q, TN)
        acc_v[:, at] = dot(key_weights, g, TN)

    x_swap(0)

    for ref in (pre, suf, w_b, w_a):
        ref[...] = jnp.zeros_like(ref)
    for step in range(1, n):
        @pl.when(s + step < n)
        def _(step=step):
            for copy in backward(step):
                copy.wait_recv()
            weight = jnp.exp(w_a[...])
            for h in range(heads):
                suf[h] += weight[h : h + 1, :] * qst[step - 1, h].astype(F32)
            w_a[...] += tot_a[step - 1]

    scale = 1.0 / DH

    def relay(way, part, hop):
        step = 1 if way == 0 else n - 1
        have = hop if way == 0 else (n - hop) % n
        give = hop + 1 if way == 0 else n - hop - 1
        return pltpu.make_async_remote_copy(
            src_ref=gg.at[part, have], dst_ref=gg.at[part, give],
            send_sem=g_send.at[way, part, hop], recv_sem=g_recv.at[way, part, hop],
            device_id={"seq": lax.rem(s + step, n)}, device_id_type=MESH,
        )

    def sends(way, hop):
        if way == 0:
            return jnp.logical_and(s >= hop, s + 1 < n)
        return jnp.logical_and(s + hop < n, s >= 1)

    def gets(way, hop):
        return s >= hop + 1 if way == 0 else s + hop + 1 < n

    def pass_on(part, hop):
        for way in range(2):
            @pl.when(gets(way, hop))
            def _(way=way):
                relay(way, part, hop).wait_recv()

            if hop + 1 < n - 1:
                @pl.when(sends(way, hop + 1))
                def _(way=way):
                    relay(way, part, hop + 1).start()

    for part in range(parts):
        for i in range(group):
            h = (part % GROUPS) * group + i
            at = pl.ds(h * DH, DH)
            cum = cum_s[h]
            to_end = jnp.exp(cum[length - 1 : length, :] - cum)
            low_suffix = suf[h].astype(BF16)
            if part < GROUPS:
                carried = to_end * dot(v_ref[:, at], low_suffix, NT)
                result = ((acc_k[:, at] + carried) * scale).astype(BF16)
                gk_ref[:, at] = result
            else:
                carried = to_end * dot(k_ref[:, at], low_suffix, NN)
                result = ((acc_v[:, at] + carried) * scale).astype(BF16)
                gv_ref[:, at] = result
            gg[part, 0, :, i * DH : (i + 1) * DH] = result
        for way in range(2):
            @pl.when(sends(way, 0))
            def _(way=way, part=part):
                relay(way, part, 0).start()


    low = lax.rem(d, 2)
    own_row = low * size
    far_row = (1 - low) * size

    def product(start, part):
        rows = rxt[pl.ds(pl.multiple_of(start, 16), size), :]
        return dot(rows, gg[part].reshape(n * length, wide), NN)

    def exchange(src, dst, send_sem, recv_sem, to):
        return pltpu.make_async_remote_copy(
            src_ref=src, dst_ref=dst, send_sem=send_sem, recv_sem=recv_sem,
            device_id={"dp": to}, device_id_type=MESH,
        )

    def level_up(level, part, i):
        levels[level, part, i] = exchange(
            lev_send.at[level, part, i], lev_recv.at[level, part, i],
            l_send.at[level, part, i], l_recv.at[level, part, i], partner(level + 1),
        )
        levels[level, part, i].start()

    halves, levels, finals = {}, {}, {}

    def multiply(i, part):
        half_send[part, i] = product(far_row + i * piece, part).astype(BF16)
        halves[part, i] = exchange(
            half_send.at[part, i], half_recv.at[part, i],
            c_send.at[part, i], c_recv.at[part, i], near,
        )
        halves[part, i].start()
        total = product(own_row + i * piece, part)
        halves[part, i].wait_recv()
        total = total + half_recv[part, i].astype(F32)
        lev_send[0, part, i] = total.astype(BF16)
        level_up(0, part, i)

    pass_on(0, 0)
    x_own.wait()
    x_turn(0)
    for wave in range(1, parts + n - 2):
        for part in range(parts):
            if 0 <= wave - part < n - 1:
                pass_on(part, wave - part)
        if wave == n - 2:
            for i in range(1, PIECES):
                x_swap(i)
        if wave >= n - 2:
            multiply(0, wave - (n - 2))
    for i in range(1, PIECES):
        x_turn(i)
        for part in range(parts):
            multiply(i, part)

    for step in range(1, n):
        @pl.when(s >= step)
        def _(step=step):
            for copy in forward(step):
                copy.wait_recv()
            weight = jnp.exp(w_b[...])
            for h in range(heads):
                pre[h] += weight[h : h + 1, :] * kst[step - 1, h].astype(F32)
            w_b[...] += tot_b[step - 1]
    for h in range(heads):
        at = pl.ds(h * DH, DH)
        carried = jnp.exp(cum_s[h]) * dot(g_ref[:, at], pre[h].astype(BF16), NT)
        gq_ref[:, at] = ((acc_q[:, at] + carried) * scale).astype(BF16)

    for level in range(bits - 1):
        for i in range(PIECES):
            for part in range(parts):
                levels[level, part, i].wait_recv()
                total = lev_send[level, part, i].astype(F32) + lev_recv[level, part, i].astype(F32)
                if level < bits - 2:
                    lev_send[level + 1, part, i] = total.astype(BF16)
                    level_up(level + 1, part, i)
                    continue
                here = outs[part // GROUPS].at[
                    pl.ds(pl.multiple_of(own_row + i * piece, 16), size),
                    pl.ds((part % GROUPS) * wide, wide),
                ]
                here[...] = (total * factor).astype(BF16)
                finals[part, i] = exchange(
                    here, here, f_send.at[part, i], f_recv.at[part, i], near
                )
                finals[part, i].start()

    for step in range(1, n):
        @pl.when(s + step < n)
        def _(step=step):
            for copy in forward(step):
                copy.wait_send()

        @pl.when(s >= step)
        def _(step=step):
            for copy in backward(step):
                copy.wait_send()
    for hop in range(n - 1):
        for way in range(2):
            @pl.when(sends(way, hop))
            def _(way=way, hop=hop):
                for part in range(parts):
                    relay(way, part, hop).wait_send()
    for copies in (x_copies, x_swaps, halves, levels):
        for copy in copies.values():
            copy.wait_send()
    for copy in finals.values():
        copy.wait()


def per_device(layer_input, queries, key_rows, value_rows, grad_out, log_decay):
    n = lax.axis_size("seq")
    dp = lax.axis_size("dp")
    bits = dp.bit_length() - 1
    length, width = queries.shape[1:]
    heads = log_decay.shape[2]
    features = layer_input.shape[2]
    cols = features // n
    size = cols // PIECES // 2
    parts = 2 * GROUPS
    wide = width // GROUPS
    tot_rows = -(-heads // 8) * 8
    factor = 1.0 / math.sqrt(dp * n * length)
    vmem = pl.BlockSpec(memory_space=pltpu.VMEM)
    dma = pltpu.SemaphoreType.DMA
    tile = (heads, DH, DH)
    grads = pl.pallas_call(
        functools.partial(kernel, n, bits, heads, factor),
        out_shape=[jax.ShapeDtypeStruct((length, width), BF16)] * 3
        + [jax.ShapeDtypeStruct((cols, width), BF16)] * 2,
        in_specs=[pl.BlockSpec(memory_space=pltpu.HBM)] * 5 + [vmem],
        out_specs=[vmem] * 5,
        scratch_shapes=[pltpu.VMEM((length, width), BF16)] * 4
        + [
            pltpu.VMEM((heads, length, DH), F32),
            pltpu.VMEM((tot_rows, DH), F32),
            pltpu.VMEM(tile, BF16),
            pltpu.VMEM(tile, BF16),
            pltpu.VMEM((n - 1,) + tile, BF16),
            pltpu.VMEM((n - 1,) + tile, BF16),
            pltpu.VMEM((n - 1, tot_rows, DH), F32),
            pltpu.VMEM((n - 1, tot_rows, DH), F32),
            pltpu.VMEM((tot_rows, DH), F32),
            pltpu.VMEM((tot_rows, DH), F32),
            pltpu.VMEM(tile, F32),
            pltpu.VMEM(tile, F32),
            pltpu.VMEM((length, width), F32),
            pltpu.VMEM((length, width), F32),
            pltpu.VMEM((length, width), F32),
            pltpu.VMEM((n, length, cols), BF16),
            pltpu.VMEM((cols, n * length), BF16),
            pltpu.VMEM((parts, n, length, wide), BF16),
            pltpu.VMEM((parts, PIECES, size, wide), BF16),
            pltpu.VMEM((parts, PIECES, size, wide), BF16),
            pltpu.VMEM((bits - 1, parts, PIECES, size, wide), BF16),
            pltpu.VMEM((bits - 1, parts, PIECES, size, wide), BF16),
            dma((4,)), dma((4, n - 1)), dma((4, n - 1)),
            dma((PIECES, n - 1)), dma((PIECES, n - 1)),
            dma((PIECES, n - 1)), dma((PIECES, n - 1)), dma,
            dma((2, parts, n - 1)), dma((2, parts, n - 1)),
            dma((parts, PIECES)), dma((parts, PIECES)),
            dma((bits - 1, parts, PIECES)), dma((bits - 1, parts, PIECES)),
            dma((parts, PIECES)), dma((parts, PIECES)),
        ],
        compiler_params=pltpu.CompilerParams(
            collective_id=0, has_side_effects=True, vmem_limit_bytes=48 << 20
        ),
    )(layer_input[0], queries[0], key_rows[0], value_rows[0], grad_out[0], log_decay[0])
    return (grads[0][None], grads[1][None], grads[2][None], grads[3], grads[4])


def solution(mesh):
    return jax.shard_map(
        per_device,
        mesh=mesh,
        in_specs=(
            P("dp", "seq", None),
            P("dp", "seq", "head"),
            P("dp", "seq", "head"),
            P("dp", "seq", "head"),
            P("dp", "seq", "head"),
            P("dp", "seq", "head"),
        ),
        out_specs=(
            P("dp", "seq", "head"),
            P("dp", "seq", "head"),
            P("dp", "seq", "head"),
            P("seq", "head"),
            P("seq", "head"),
        ),
        check_vma=False,
    )
```
